32 devices in a mesh: section: 4 (over z), expert: 8 (over y, x, core).
Axes of the slice: x: 2, y: 2, z: 4, core: 2. Of those that a mesh axis runs over, the one named last changes fastest.
Arguments:
- hidden_fwd: bfloat16 [4, 2048, 1536], P('section', 'expert'), may hold values from -6 to 6
- down_weight: bfloat16 [8, 1536, 2048], P('expert'), may hold values from -0.15625 to 0.15625
- residual: bfloat16 [4, 256, 2048], P('section', 'expert'), may hold values from -6 to 6
- route_fwd: int32 [4, 256, 8], P('section', 'expert'), may hold values from 0 to 255, as said below
- gate_fwd: float32 [4, 256, 8], P('section', 'expert'), may hold values from 0.05 to 0.35
- hidden_bwd: bfloat16 [4, 2048, 1536], P('section', 'expert'), may hold values from -0.59765625 to 0.59765625
- route_bwd: int32 [4, 256, 8], P('section', 'expert'), may hold values from 0 to 255, as said below
- gate_bwd: float32 [4, 256, 8], P('section', 'expert'), may hold values from 0.05 to 0.35
- upstream: bfloat16 [4, 256, 2048], P('section', 'expert'), may hold values from -3 to 3
Outputs:
- next_input: bfloat16 [4, 256, 2048], P('section', 'expert')
- hidden_grad: bfloat16 [4, 2048, 1536], P('section', 'expert')
- gate_grad: float32 [4, 2048], P('section', 'expert')
The draws below stay inside these ranges and needn't reach their ends.
Inputs may be any that keep to these rules, and one draw needn't show every extreme that they name: `route_fwd`: for each section, the 256 entries of the tokens of one device are all different; entry // 32 names the expert and entry % 32 a position among that device's rows for it, so every expert receives exactly 32 routes from each device on each section; the 8 entries of a token name different experts. `route_bwd`: same law as route_fwd, drawn independently.
All inputs are finite; a program needn't handle non-finite values.
Results may differ from the reference program's by a relative error of at most 0.0051.
Values may be sent and summed in bfloat16 or wider, within the bound.
A program may use at most 64 MiB of HBM per device.

```python
import jax
import jax.numpy as jnp
from jax import lax

D = 2048
TOP = 8
FF = 1536
TOK_DEV = 32
EXPERTS = 8
SECTIONS = 4
ROUTES_DEV = 256
CAP = 32
TOKENS = 256
ROUTES = 2048


def routing_table(key):
    block_keys = jax.random.split(key, SECTIONS * EXPERTS)

    def one_block(block_key):
        token_key, expert_key = jax.random.split(block_key)
        token_order = jax.random.permutation(token_key, TOK_DEV)
        expert_order = jax.random.permutation(expert_key, EXPERTS)
        placed = token_order[:, None] * TOP + jnp.arange(TOP, dtype=jnp.int32)[None, :]
        expert_id = expert_order[placed % EXPERTS]
        rank_in = placed // EXPERTS
        return expert_id * CAP + rank_in
    tables = jax.vmap(one_block)(block_keys)
    return tables.reshape(SECTIONS, TOKENS, TOP).astype(jnp.int32)


def draw_route_fwd(key, part):
    return routing_table(jax.random.fold_in(key, 11))


def draw_route_bwd(key, part):
    return routing_table(jax.random.fold_in(key, 23))


def steps_of(stream_key, extent, pieces, smallest, top_value):
    level = 1.0
    for dim, shards_of in pieces:
        draws = jax.random.uniform(jax.random.fold_in(jax.random.fold_in(stream_key, 6), dim), (shards_of,), jnp.float32, smallest / len(pieces), top_value / len(pieces))
        level = level * jnp.repeat(jnp.exp(draws), extent[dim] // shards_of).reshape((-1,) + (1,) * (len(extent) - 1 - dim))
    return level


def gaussian(rng, dims, width, most, shards=(), held_as=jnp.bfloat16):
    drawn = jax.random.normal(rng, dims, jnp.float32) * width
    if len(shards) > 0:
        drawn = steps_of(rng, dims, shards, -0.22, 0.18) * drawn
    return jnp.clip(drawn, min=-most, max=most).astype(held_as)


def setup_inputs(seed: int = 0) -> dict:
    streams_of = jax.random.split(jax.random.key(seed), 10)
    hidden_fwd = gaussian(streams_of[0], (SECTIONS, ROUTES, FF), 1.0, 6.0, ((0, 4), (1, 8)))
    down_weight = gaussian(streams_of[1], (EXPERTS, FF, D), FF ** -0.5, 0.15625, ((0, 8),))
    residual = gaussian(streams_of[2], (SECTIONS, TOKENS, D), 1.0, 6.0, ((0, 4), (1, 8)))
    route_fwd = draw_route_fwd(jax.random.fold_in(streams_of[9], 71), 0)
    gate_fwd = jnp.clip(0.05 + 0.29999999 * jax.random.uniform(streams_of[4], (SECTIONS, TOKENS, TOP), jnp.float32) ** steps_of(streams_of[4], (SECTIONS, TOKENS, TOP), ((0, 4), (1, 8)), -0.2, 0.2), 0.05, 0.35)
    hidden_bwd = gaussian(streams_of[5], (SECTIONS, ROUTES, FF), 0.1, 0.59765625, ((0, 4), (1, 8)))
    route_bwd = draw_route_bwd(jax.random.fold_in(streams_of[9], 71), 0)
    gate_bwd = jnp.clip(0.05 + 0.29999999 * jax.random.uniform(streams_of[7], (SECTIONS, TOKENS, TOP), jnp.float32) ** steps_of(streams_of[7], (SECTIONS, TOKENS, TOP), ((0, 4), (1, 8)), -0.2, 0.2), 0.05, 0.35)
    upstream = gaussian(streams_of[8], (SECTIONS, TOKENS, D), 0.5, 3.0, ((0, 4), (1, 8)))
    return dict(hidden_fwd=hidden_fwd, down_weight=down_weight, residual=residual, route_fwd=route_fwd, gate_fwd=gate_fwd, hidden_bwd=hidden_bwd, route_bwd=route_bwd, gate_bwd=gate_bwd, upstream=upstream)


def destination(route_slot):
    source_dev = (jnp.arange(TOKENS, dtype=jnp.int32) // TOK_DEV)[:, None]
    expert_id = route_slot // CAP
    rank_in = route_slot % CAP
    return expert_id * ROUTES_DEV + source_dev * CAP + rank_in


def forward_section(section_parts, down_weight):
    hidden, route_slot, gate, residual = section_parts
    hidden_blocks = hidden.reshape(EXPERTS, ROUTES_DEV, FF)

    def project(pair):
        block, matrix = pair
        return jnp.dot(block, matrix, preferred_element_type=jnp.float32).astype(jnp.bfloat16)

    expert_out = lax.map(project, (hidden_blocks, down_weight)).reshape(ROUTES, D)
    picked_rows = expert_out[destination(route_slot)].astype(jnp.float32)
    combined = residual.astype(jnp.float32) + jnp.sum(gate[:, :, None] * picked_rows, axis=1)
    return combined.astype(jnp.bfloat16)


def backward_section(section_parts, down_weight):
    hidden, route_slot, gate, grad_in = section_parts
    destination_rows = destination(route_slot).reshape(-1)
    anchor = jnp.zeros((ROUTES,), jnp.int32).at[destination_rows].set(jnp.arange(ROUTES, dtype=jnp.int32))
    token_id = anchor // TOP
    grad_rows = grad_in[token_id]
    weight_rows = lax.optimization_barrier(gate.reshape(-1)[anchor].astype(jnp.bfloat16)).astype(jnp.float32)

    def per_expert(group):
        grad_block, hidden_block, weight_block, matrix = group
        grad_hidden = jnp.dot(grad_block, matrix.T, preferred_element_type=jnp.float32)
        gate_grad = jnp.sum(hidden_block.astype(jnp.float32) * grad_hidden, axis=1)
        hidden_grad = (weight_block[:, None] * grad_hidden).astype(jnp.bfloat16)
        return hidden_grad, gate_grad

    hidden_grad, gate_grad = lax.map(per_expert, (grad_rows.reshape(EXPERTS, ROUTES_DEV, D), hidden.reshape(EXPERTS, ROUTES_DEV, FF), weight_rows.reshape(EXPERTS, ROUTES_DEV), down_weight))
    return hidden_grad.reshape(ROUTES, FF), gate_grad.reshape(ROUTES)


def reference(hidden_fwd, down_weight, residual, route_fwd, gate_fwd, hidden_bwd, route_bwd, gate_bwd, upstream):
    def run_forward(section_parts):
        return forward_section(section_parts, down_weight)

    def run_backward(section_parts):
        return backward_section(section_parts, down_weight)

    layer_out = lax.map(run_forward, (hidden_fwd, route_fwd, gate_fwd, residual))
    next_input = jnp.roll(layer_out, 1, axis=0)
    grad_in = jnp.roll(upstream, -1, axis=0)
    hidden_grad, gate_grad = lax.map(run_backward, (hidden_bwd, route_bwd, gate_bwd, grad_in))
    return next_input, hidden_grad, gate_grad
```

```python
import functools

import jax
import jax.numpy as jnp
from jax import lax
from jax.experimental import pallas as pl
from jax.experimental.pallas import tpu as pltpu
from jax.sharding import PartitionSpec as P

F32 = jnp.float32
BF16 = jnp.bfloat16


def from_behind(block, axis, distance):
    devices = range(lax.axis_size(axis))
    route = [((i - distance) % len(devices), i) for i in devices]
    return lax.ppermute(block, axis, route)


def forward_local(hidden_fwd, down_weight):
    return jnp.dot(hidden_fwd[0], down_weight[0], preferred_element_type=F32).astype(BF16)


def combine_rows(returned, route_fwd, gate_fwd, residual):
    picked_rows = returned[route_fwd[0]]
    combined = residual[0].astype(F32) + jnp.sum(gate_fwd[0][:, :, None] * picked_rows, axis=1)
    return combined.astype(BF16)


def dispatch_rows(grad_in, route_bwd, gate_bwd):
    top = route_bwd.shape[-1]
    flat_slots = route_bwd[0].reshape(-1)
    route_count = flat_slots.shape[0]
    anchor = (
        jnp.zeros((route_count,), jnp.int32)
        .at[flat_slots]
        .set(jnp.arange(route_count, dtype=jnp.int32))
    )
    outgoing = grad_in[0][anchor // top]
    weight_rows = gate_bwd[0].reshape(-1)[anchor].astype(BF16)
    return (outgoing, weight_rows)


def backward_local(received, weights_in, hidden_bwd, down_weight):
    grad_hidden = lax.dot_general(
        received, down_weight[0], (((1,), (1,)), ((), ())), preferred_element_type=F32
    )
    gate_grad = jnp.sum(hidden_bwd[0] * grad_hidden, axis=1)
    hidden_grad = (weights_in.astype(F32)[:, None] * grad_hidden).astype(BF16)
    return (hidden_grad[None], gate_grad[None])


def sparse_body(
    hidden_fwd, down_weight, residual, route_fwd, gate_fwd, hidden_bwd, route_bwd, gate_bwd, upstream
):
    grad_in = from_behind(upstream, "section", -1)
    outgoing, weight_rows = dispatch_rows(grad_in, route_bwd, gate_bwd)
    projected = forward_local(hidden_fwd, down_weight)
    returned = lax.all_to_all(projected, "expert", split_axis=0, concat_axis=0, tiled=True)
    received, weights_in = (
        lax.all_to_all(outgoing, "expert", split_axis=0, concat_axis=0, tiled=True),
        lax.all_to_all(weight_rows, "expert", split_axis=0, concat_axis=0, tiled=True),
    )
    layer_out = combine_rows(returned, route_fwd, gate_fwd, residual)
    next_input = from_behind(layer_out[None], "section", 1)
    hidden_grad, gate_grad = backward_local(received, weights_in, hidden_bwd, down_weight)
    return (next_input, hidden_grad, gate_grad)


def kernel(
    n, sections, nch, nbw,
    hf_ref, w_ref, res_ref, rf_ref, gf_ref, hb_ref, rb_ref, gb_ref, up_ref,
    next_ref, hg_ref, gg_ref,
    hf, w, res, hb, rt, gt, gbuf, gp, cown, csend, crecv, ssend, srecv, nout, hgs,
    ld, sm_loc, sm_send, sm_recv, z_send, z_recv, ag_send, ag_recv, fw_send, fw_recv,
    xc_send, xc_recv, rs_send, rs_recv, no_send, no_recv, out_sem,
):
    e = lax.axis_index("expert")
    s = lax.axis_index("section")
    chips = n // 2
    p = lax.div(e, 2)
    c = lax.rem(e, 2)
    mine = c * chips + p
    partner = e + 1 - 2 * c
    above = lax.rem(s + 1, sections)
    below = lax.rem(s + sections - 1, sections)
    rows, ff = hf.shape
    d = w.shape[1]
    tokens = res.shape[0]
    cap = rows // n
    half = chips * tokens
    dc = d // nch
    fb = ff // nbw

    def cols(i):
        return slice(i * dc, (i + 1) * dc)

    def remote(src, dst, ss, rs, section=None, expert=None):
        return pltpu.make_async_remote_copy(
            src_ref=src, dst_ref=dst, send_sem=ss, recv_sem=rs,
            device_id={
                "section": s if section is None else section,
                "expert": e if expert is None else expert,
            },
            device_id_type=pl.DeviceIdType.MESH,
        )

    loads = [pltpu.make_async_copy(hf_ref.at[0], hf, ld.at[nch])]
    for i in range(nch):
        loads.append(
            pltpu.make_async_copy(w_ref.at[0, :, cols(i)], w.at[:, cols(i)], ld.at[i])
        )
    loads.append(pltpu.make_async_copy(res_ref.at[0], res, ld.at[nch + 1]))
    loads.append(pltpu.make_async_copy(hb_ref.at[0], hb, ld.at[nch + 2]))
    for load in loads:
        load.start()
    tables = [(rf_ref, rt, 0), (gf_ref, gt, 0), (rb_ref, rt, 1), (gb_ref, gt, 1)]
    local = []
    for i, (src, dst, kind) in enumerate(tables):
        local.append(pltpu.make_async_copy(src, dst.at[kind, mine], sm_loc.at[i]))
        local[-1].start()

    barrier = pltpu.get_barrier_semaphore()
    for k in range(1, n):
        pl.semaphore_signal(
            barrier, inc=1, device_id={"section": s, "expert": lax.rem(e + k, n)},
            device_id_type=pl.DeviceIdType.MESH,
        )
    for other in (above, below):
        pl.semaphore_signal(
            barrier, inc=1, device_id={"section": other, "expert": e},
            device_id_type=pl.DeviceIdType.MESH,
        )
    pl.semaphore_wait(barrier, n + 1)

    zs = []
    for i in range(nch):
        zs.append(
            remote(up_ref.at[0, :, cols(i)], gbuf.at[c, p, :, cols(i)],
                   z_send.at[i], z_recv.at[i], section=below)
        )
        zs[-1].start()
    small = []
    for i, (src, dst, kind) in enumerate(tables):
        for k in range(1, n):
            small.append(
                remote(src, dst.at[kind, mine], sm_send.at[i, k - 1], sm_recv.at[i, k - 1],
                       expert=lax.rem(e + k, n))
            )
            small[-1].start()

    drains = []

    def send(copy):
        copy.start()
        drains.append(copy)
        return copy

    def peer(k):
        return 2 * lax.rem(p + k, chips) + c

    def gather_out(i):
        zs[i].wait_recv()
        block = gbuf.at[c, p, :, cols(i)]
        for k in range(1, chips):
            send(remote(block, block, ag_send.at[k - 1, i], ag_recv.at[k - 1, i], expert=peer(k)))
        send(remote(block, block, fw_send.at[0, i], fw_recv.at[0, i], expert=partner))

    def gather_forward(k, i):
        block = gbuf.at[c, lax.rem(p + chips - k, chips), :, cols(i)]
        remote(block, block, ag_send.at[k - 1, i], ag_recv.at[k - 1, i], expert=partner).wait_recv()
        send(remote(block, block, fw_send.at[k, i], fw_recv.at[k, i], expert=partner))

    def gather_done(k, i):
        block = gbuf.at[1 - c, lax.rem(p + chips - k, chips), :, cols(i)]
        remote(block, block, fw_send.at[k, i], fw_recv.at[k, i], expert=partner).wait_recv()

    def project(i):
        loads[1 + i].wait()
        return jnp.dot(hf[...], w[:, cols(i)], preferred_element_type=F32).astype(BF16)

    loads[0].wait()
    out = project(0)

    for copy in local:
        copy.wait()
    for copy in small:
        copy.wait_recv()

    def table(ref, kind):
        return jnp.concatenate([ref[kind, q] for q in range(n)], axis=1)

    lo = e * cap
    lane = lax.broadcasted_iota(jnp.int32, (1, n * tokens), 1)
    lane_q = lane // tokens
    lane_base = (2 * (lane_q % chips) + lane_q // chips) * cap

    route = table(rt, 0)
    hit = (route >= lo) & (route < lo + cap)
    pos = jnp.where(hit, route - lo, 0).astype(F32).T
    gate_col = jnp.sum(jnp.where(hit, table(gt, 0), 0.0).T, axis=1, keepdims=True)
    row = lax.broadcasted_iota(jnp.int32, (n * tokens, 1), 0)
    row_q = row // tokens
    want = (2 * (row_q % chips) + row_q // chips) * cap + jnp.sum(
        pos, axis=1, keepdims=True
    ).astype(jnp.int32)
    pick = jnp.where(
        lax.broadcasted_iota(jnp.int32, (n * tokens, rows), 1) == want, 1.0, 0.0
    ).astype(BF16)

    def weigh(i, out):
        got = gate_col * jnp.dot(pick, out, preferred_element_type=F32)
        low, high = got[:half], got[half:]
        cown[:, cols(i)] = jnp.where(c == 0, low, high)
        csend[:, cols(i)] = jnp.where(c == 0, high, low).astype(BF16)
        return send(
            remote(csend.at[:, cols(i)], crecv.at[:, cols(i)], xc_send.at[i], xc_recv.at[i],
                   expert=partner)
        )

    pairs = []
    for i in range(nch):
        if i:
            out = project(i)
        pairs.append(weigh(i, out))
        gather_out(i)

    rs = {}
    for i in range(nch):
        pairs[i].wait_recv()
        total = cown[:, cols(i)] + crecv[:, cols(i)].astype(F32)
        cown[:, cols(i)] = total
        for q in range(chips):
            ssend[q, :, cols(i)] = total[q * tokens:(q + 1) * tokens].astype(BF16)
        for k in range(1, chips):
            rs[k, i] = send(
                remote(ssend.at[lax.rem(p + k, chips), :, cols(i)],
                       srecv.at[k - 1, :, cols(i)],
                       rs_send.at[k - 1, i], rs_recv.at[k - 1, i], expert=peer(k))
            )

    for i in range(nch):
        for k in range(1, chips):
            gather_forward(k, i)

    route = table(rt, 1)
    hit = (route >= lo) & (route < lo + cap)
    slot = jnp.sum(jnp.where(hit, route - lo, 0), axis=0, keepdims=True)
    gate_row = jnp.sum(jnp.where(hit, table(gt, 1), 0.0), axis=0, keepdims=True)
    match = lax.broadcasted_iota(jnp.int32, (rows, n * tokens), 0) == lane_base + slot
    weight_col = jnp.sum(jnp.where(match, gate_row, 0.0), axis=1, keepdims=True)
    weight_col = weight_col.astype(BF16).astype(F32)
    place = jnp.where(match, 1.0, 0.0).astype(BF16)

    for i in range(nch):
        for k in range(chips):
            gather_done(k, i)
        tok = gbuf[:, :, :, cols(i)].reshape(n * tokens, dc)
        gp[:, cols(i)] = jnp.dot(place, tok, preferred_element_type=F32).astype(BF16)

    loads[nch + 1].wait()
    loads[nch + 2].wait()
    nos = []

    def finish(i):
        total = cown[pl.ds(pl.multiple_of(p * tokens, tokens), tokens), cols(i)]
        total = res[:, cols(i)].astype(F32) + total
        for k in range(1, chips):
            rs[k, i].wait_recv()
            total = total + srecv[k - 1, :, cols(i)].astype(F32)
        nout[:, cols(i)] = total.astype(BF16)
        nos.append(
            send(remote(nout.at[:, cols(i)], next_ref.at[0, :, cols(i)],
                        no_send.at[i], no_recv.at[i], section=above))
        )

    outs = []
    gate_sum = jnp.zeros((rows, 1), F32)
    done = 0
    for j in range(nbw):
        span = slice(j * fb, (j + 1) * fb)
        grad = lax.dot_general(
            gp[...], w[span, :], (((1,), (1,)), ((), ())), preferred_element_type=F32
        )
        gate_sum = gate_sum + jnp.sum(hb[:, span].astype(F32) * grad, axis=1, keepdims=True)
        hgs[:, span] = (weight_col * grad).astype(BF16)
        outs.append(
            pltpu.make_async_copy(hgs.at[:, span], hg_ref.at[0, :, span], out_sem.at[j])
        )
        outs[-1].start()
        if done < nch:
            finish(done)
            done += 1
    while done < nch:
        finish(done)
        done += 1
    gg_ref[...] = jnp.broadcast_to(gate_sum, (rows, 128)).T[0:1]

    for copy in nos:
        copy.wait_recv()
    for copy in outs:
        copy.wait()
    for copy in zs + small + drains:
        copy.wait_send()


def dense_body(
    hidden_fwd, down_weight, residual, route_fwd, gate_fwd, hidden_bwd, route_bwd, gate_bwd, upstream
):
    n = lax.axis_size("expert")
    sections = lax.axis_size("section")
    _, rows, ff = hidden_fwd.shape
    d = down_weight.shape[2]
    tokens, top = route_fwd.shape[1:]
    chips = n // 2
    nch, nbw = 4, 3
    half = chips * tokens
    dma = pltpu.SemaphoreType.DMA
    hbm = pl.BlockSpec(memory_space=pl.ANY)
    return pl.pallas_call(
        functools.partial(kernel, n, sections, nch, nbw),
        out_shape=(
            jax.ShapeDtypeStruct((1, tokens, d), BF16),
            jax.ShapeDtypeStruct((1, rows, ff), BF16),
            jax.ShapeDtypeStruct((1, rows), F32),
        ),
        in_specs=[hbm] * 9,
        out_specs=(hbm, hbm, pl.BlockSpec(memory_space=pltpu.VMEM)),
        scratch_shapes=[
            pltpu.VMEM((rows, ff), BF16),
            pltpu.VMEM((ff, d), BF16),
            pltpu.VMEM((tokens, d), BF16),
            pltpu.VMEM((rows, ff), BF16),
            pltpu.VMEM((2, n, top, tokens), jnp.int32),
            pltpu.VMEM((2, n, top, tokens), F32),
            pltpu.VMEM((2, chips, tokens, d), BF16),
            pltpu.VMEM((rows, d), BF16),
            pltpu.VMEM((half, d), F32),
            pltpu.VMEM((half, d), BF16),
            pltpu.VMEM((half, d), BF16),
            pltpu.VMEM((chips, tokens, d), BF16),
            pltpu.VMEM((chips - 1, tokens, d), BF16),
            pltpu.VMEM((tokens, d), BF16),
            pltpu.VMEM((rows, ff), BF16),
            dma((nch + 3,)),
            dma((4,)),
            dma((4, n - 1)),
            dma((4, n - 1)),
            dma((nch,)),
            dma((nch,)),
            dma((chips - 1, nch)),
            dma((chips - 1, nch)),
            dma((chips, nch)),
            dma((chips, nch)),
            dma((nch,)),
            dma((nch,)),
            dma((chips - 1, nch)),
            dma((chips - 1, nch)),
            dma((nch,)),
            dma((nch,)),
            dma((nbw,)),
        ],
        compiler_params=pltpu.CompilerParams(
            collective_id=0, has_side_effects=True, vmem_limit_bytes=60 << 20
        ),
    )(
        hidden_fwd, down_weight, residual, route_fwd[0].T, gate_fwd[0].T, hidden_bwd,
        route_bwd[0].T, gate_bwd[0].T, upstream,
    )


def body(*args):
    n = lax.axis_size("expert")
    dense = args[3].shape[2] == n and n % 2 == 0 and lax.axis_size("section") > 2
    return (dense_body if dense else sparse_body)(*args)


def solution(mesh):
    wide = P("section", "expert", None)
    return jax.shard_map(
        body,
        mesh=mesh,
        in_specs=(wide, P("expert", None, None), wide, wide, wide, wide, wide, wide, wide),
        out_specs=(wide, wide, P("section", "expert")),
        check_vma=False,
    )
```

```python
import functools

import jax
import jax.numpy as jnp
from jax import lax
from jax.experimental import pallas as pl
from jax.experimental.pallas import tpu as pltpu
from jax.sharding import PartitionSpec as P

F32 = jnp.float32
BF16 = jnp.bfloat16


def from_behind(block, axis, distance):
    devices = range(lax.axis_size(axis))
    route = [((i - distance) % len(devices), i) for i in devices]
    return lax.ppermute(block, axis, route)


def forward_local(hidden_fwd, down_weight):
    return jnp.dot(hidden_fwd[0], down_weight[0], preferred_element_type=F32).astype(BF16)


def combine_rows(returned, route_fwd, gate_fwd, residual):
    picked_rows = returned[route_fwd[0]]
    combined = residual[0].astype(F32) + jnp.sum(gate_fwd[0][:, :, None] * picked_rows, axis=1)
    return combined.astype(BF16)


def dispatch_rows(grad_in, route_bwd, gate_bwd):
    top = route_bwd.shape[-1]
    flat_slots = route_bwd[0].reshape(-1)
    route_count = flat_slots.shape[0]
    anchor = (
        jnp.zeros((route_count,), jnp.int32)
        .at[flat_slots]
        .set(jnp.arange(route_count, dtype=jnp.int32))
    )
    outgoing = grad_in[0][anchor // top]
    weight_rows = gate_bwd[0].reshape(-1)[anchor].astype(BF16)
    return (outgoing, weight_rows)


def backward_local(received, weights_in, hidden_bwd, down_weight):
    grad_hidden = lax.dot_general(
        received, down_weight[0], (((1,), (1,)), ((), ())), preferred_element_type=F32
    )
    gate_grad = jnp.sum(hidden_bwd[0] * grad_hidden, axis=1)
    hidden_grad = (weights_in.astype(F32)[:, None] * grad_hidden).astype(BF16)
    return (hidden_grad[None], gate_grad[None])


def sparse_body(
    hidden_fwd, down_weight, residual, route_fwd, gate_fwd, hidden_bwd, route_bwd, gate_bwd, upstream
):
    grad_in = from_behind(upstream, "section", -1)
    outgoing, weight_rows = dispatch_rows(grad_in, route_bwd, gate_bwd)
    projected = forward_local(hidden_fwd, down_weight)
    returned = lax.all_to_all(projected, "expert", split_axis=0, concat_axis=0, tiled=True)
    received, weights_in = (
        lax.all_to_all(outgoing, "expert", split_axis=0, concat_axis=0, tiled=True),
        lax.all_to_all(weight_rows, "expert", split_axis=0, concat_axis=0, tiled=True),
    )
    layer_out = combine_rows(returned, route_fwd, gate_fwd, residual)
    next_input = from_behind(layer_out[None], "section", 1)
    hidden_grad, gate_grad = backward_local(received, weights_in, hidden_bwd, down_weight)
    return (next_input, hidden_grad, gate_grad)


def kernel(
    n, sections, nch, nag, nbw,
    hf_ref, w_ref, res_ref, rf_ref, gf_ref, hb_ref, rb_ref, gb_ref, up_ref,
    next_ref, hg_ref, gg_ref,
    hf, w, res, hb, ti, tf, pack, tab, gbuf, gp, cown, csend, crecv, ssend, smid, r1a, r1b, r2,
    nout, hgs,
    ld, sm_loc, sm_send, sm_recv, z_send, z_recv, ag_send, ag_recv, fw_send, fw_recv,
    xc_send, xc_recv, rs_send, rs_recv, no_send, no_recv, out_sem,
):
    e = lax.axis_index("expert")
    s = lax.axis_index("section")
    chips = n // 2
    p = lax.div(e, 2)
    c = lax.rem(e, 2)
    mine = c * chips + p
    partner = e + 1 - 2 * c
    above = lax.rem(s + 1, sections)
    below = lax.rem(s + sections - 1, sections)
    beside_x = p + 1 - 2 * lax.rem(p, 2)
    beside_y = lax.rem(p + 2, chips)
    across = chips - 1 - p
    rows, ff = hf.shape
    d = w.shape[1]
    tokens = res.shape[0]
    cap = rows // n
    half = chips * tokens
    dc = d // nch
    ta = tokens // nag
    fb = ff // nbw

    def cols(i):
        return slice(i * dc, (i + 1) * dc)

    def part(i):
        return slice(i * ta, (i + 1) * ta)

    def of_chip(q):
        return pl.ds(pl.multiple_of(q * tokens, tokens), tokens)

    def remote(src, dst, ss, rs, section=None, expert=None):
        return pltpu.make_async_remote_copy(
            src_ref=src, dst_ref=dst, send_sem=ss, recv_sem=rs,
            device_id={
                "section": s if section is None else section,
                "expert": e if expert is None else expert,
            },
            device_id_type=pl.DeviceIdType.MESH,
        )

    barrier = pltpu.get_barrier_semaphore()
    for k in range(1, n):
        pl.semaphore_signal(
            barrier, inc=1, device_id={"section": s, "expert": lax.rem(e + k, n)},
            device_id_type=pl.DeviceIdType.MESH,
        )
    for other in (above, below):
        pl.semaphore_signal(
            barrier, inc=1, device_id={"section": other, "expert": e},
            device_id_type=pl.DeviceIdType.MESH,
        )
    local = []
    for i, (src, dst) in enumerate(
        [(rf_ref, ti.at[0]), (gf_ref, tf.at[0]), (rb_ref, ti.at[1]), (gb_ref, tf.at[1])]
    ):
        local.append(pltpu.make_async_copy(src, dst, sm_loc.at[i]))
        local[-1].start()
    loads = [pltpu.make_async_copy(hf_ref.at[0], hf, ld.at[nch])]
    for i in range(nch):
        loads.append(
            pltpu.make_async_copy(w_ref.at[0, :, cols(i)], w.at[:, cols(i)], ld.at[i])
        )
    loads.append(pltpu.make_async_copy(res_ref.at[0], res, ld.at[nch + 1]))
    loads.append(pltpu.make_async_copy(hb_ref.at[0], hb, ld.at[nch + 2]))
    for load in loads:
        load.start()
    for copy in local:
        copy.wait()
    packed = jnp.concatenate([ti[0].astype(F32), tf[0], ti[1].astype(F32), tf[1]], axis=1)
    pack[...] = packed
    tab[mine] = packed
    pl.semaphore_wait(barrier, n + 1)

    drains = []

    def send(copy):
        copy.start()
        drains.append(copy)
        return copy

    zs = []
    for i in range(nag):
        zs.append(
            send(remote(up_ref.at[0, part(i)], gbuf.at[c, p, part(i)],
                        z_send.at[i], z_recv.at[i], section=below))
        )
    small = []
    for k in range(1, n):
        small.append(
            send(remote(pack, tab.at[mine], sm_send.at[k - 1], sm_recv.at[k - 1],
                        expert=lax.rem(e + k, n)))
        )

    def expert_at(q):
        return 2 * q + c

    def block(q, i, core=None):
        return gbuf.at[c if core is None else core, q, part(i)]

    def gather(q, j, i, to):
        ref = block(q, i)
        return remote(ref, ref, ag_send.at[j, i], ag_recv.at[j, i], expert=expert_at(to))

    def hand_over(q, j, i, core=None):
        ref = block(q, i, core)
        return remote(ref, ref, fw_send.at[j, i], fw_recv.at[j, i], expert=partner)

    def gather_out(i):
        zs[i].wait_recv()
        send(gather(p, 0, i, beside_x))
        send(gather(p, 1, i, beside_y))
        send(hand_over(p, 0, i))

    def gather_near(i):
        gather(beside_x, 0, i, beside_x).wait_recv()
        if i % 2 == 0:
            send(gather(beside_x, 2, i, beside_y))
        send(hand_over(beside_x, 1, i))
        gather(beside_y, 1, i, beside_y).wait_recv()
        if i % 2 == 1:
            send(gather(beside_y, 2, i, beside_x))
        send(hand_over(beside_y, 2, i))

    def gather_far(i):
        gather(across, 2, i, beside_x).wait_recv()
        send(hand_over(across, 3, i))

    def gather_done(i):
        for j, q in enumerate((p, beside_x, beside_y, across)):
            hand_over(q, j, i, 1 - c).wait_recv()

    def project(i):
        loads[1 + i].wait()
        return jnp.dot(hf[...], w[:, cols(i)], preferred_element_type=F32).astype(BF16)

    loads[0].wait()
    out = project(0)
    for copy in small:
        copy.wait_recv()

    def table(kind):
        span = slice(kind * tokens, (kind + 1) * tokens)
        return jnp.concatenate([tab[q, :, span] for q in range(n)], axis=1)

    lo = e * cap
    lane = lax.broadcasted_iota(jnp.int32, (1, n * tokens), 1)
    lane_q = lane // tokens
    lane_base = (2 * (lane_q % chips) + lane_q // chips) * cap

    route = table(0).astype(jnp.int32)
    hit = (route >= lo) & (route < lo + cap)
    pos = jnp.where(hit, route - lo, 0).astype(F32).T
    gate_col = jnp.sum(jnp.where(hit, table(1), 0.0).T, axis=1, keepdims=True)
    row = lax.broadcasted_iota(jnp.int32, (n * tokens, 1), 0)
    row_q = row // tokens
    want = (2 * (row_q % chips) + row_q // chips) * cap + jnp.sum(
        pos, axis=1, keepdims=True
    ).astype(jnp.int32)
    pick = jnp.where(
        lax.broadcasted_iota(jnp.int32, (n * tokens, rows), 1) == want, 1.0, 0.0
    ).astype(BF16)

    def weigh(i, out):
        got = gate_col * jnp.dot(pick, out, preferred_element_type=F32)
        low, high = got[:half], got[half:]
        cown[:, cols(i)] = jnp.where(c == 0, low, high)
        csend[:, cols(i)] = jnp.where(c == 0, high, low).astype(BF16)
        return send(
            remote(csend.at[:, cols(i)], crecv.at[:, cols(i)], xc_send.at[i], xc_recv.at[i],
                   expert=partner)
        )

    def first_second(i):
        return (beside_x, beside_y) if i % 2 == 0 else (beside_y, beside_x)

    far, near, last, nos = {}, {}, {}, []

    def scatter_out(i):
        first, _ = first_second(i)
        pairs[i].wait_recv()
        total = cown[:, cols(i)] + crecv[:, cols(i)].astype(F32)
        cown[:, cols(i)] = total
        ssend[:, cols(i)] = total.astype(BF16)
        far[i] = send(remote(ssend.at[of_chip(across), cols(i)], r1a.at[:, cols(i)],
                             rs_send.at[0, i], rs_recv.at[0, i], expert=expert_at(first)))
        near[i] = send(remote(ssend.at[of_chip(first), cols(i)], r1b.at[:, cols(i)],
                              rs_send.at[1, i], rs_recv.at[1, i], expert=expert_at(first)))

    def scatter_mid(i):
        _, second = first_second(i)
        far[i].wait_recv()
        both = cown[of_chip(second), cols(i)] + r1a[:, cols(i)].astype(F32)
        smid[:, cols(i)] = both.astype(BF16)
        last[i] = send(remote(smid.at[:, cols(i)], r2.at[:, cols(i)],
                              rs_send.at[2, i], rs_recv.at[2, i], expert=expert_at(second)))

    def finish(i):
        near[i].wait_recv()
        total = res[:, cols(i)].astype(F32) + cown[of_chip(p), cols(i)]
        total = total + r1b[:, cols(i)].astype(F32)
        last[i].wait_recv()
        total = total + r2[:, cols(i)].astype(F32)
        nout[:, cols(i)] = total.astype(BF16)
        nos.append(
            send(remote(nout.at[:, cols(i)], next_ref.at[0, :, cols(i)],
                        no_send.at[i], no_recv.at[i], section=above))
        )

    pairs = []
    for i in range(nch):
        if i:
            out = project(i)
        pairs.append(weigh(i, out))
        if i >= 1:
            scatter_out(i - 1)
        if i < nag:
            gather_out(i)
    scatter_out(nch - 1)
    for i in range(nag):
        gather_near(i)
    for i in range(nch):
        scatter_mid(i)
    for i in range(nag):
        gather_far(i)

    route = table(2).astype(jnp.int32)
    hit = (route >= lo) & (route < lo + cap)
    slot = jnp.sum(jnp.where(hit, route - lo, 0), axis=0, keepdims=True)
    gate_row = jnp.sum(jnp.where(hit, table(3), 0.0), axis=0, keepdims=True)
    match = lax.broadcasted_iota(jnp.int32, (rows, n * tokens), 0) == lane_base + slot
    weight_col = jnp.sum(jnp.where(match, gate_row, 0.0), axis=1, keepdims=True)
    weight_col = weight_col.astype(BF16).astype(F32)
    place = jnp.where(match, 1.0, 0.0).astype(BF16)

    loads[nch + 1].wait()
    loads[nch + 2].wait()
    for i in range(nch):
        finish(i)
    for i in range(nag):
        gather_done(i)
    for i in range(nch):
        tok = gbuf[:, :, :, cols(i)].reshape(n * tokens, dc)
        gp[:, cols(i)] = jnp.dot(place, tok, preferred_element_type=F32).astype(BF16)

    outs = []
    gate_sum = jnp.zeros((rows, 1), F32)
    for j in range(nbw):
        span = slice(j * fb, (j + 1) * fb)
        grad = lax.dot_general(
            gp[...], w[span, :], (((1,), (1,)), ((), ())), preferred_element_type=F32
        )
        gate_sum = gate_sum + jnp.sum(hb[:, span].astype(F32) * grad, axis=1, keepdims=True)
        hgs[:, span] = (weight_col * grad).astype(BF16)
        outs.append(
            pltpu.make_async_copy(hgs.at[:, span], hg_ref.at[0, :, span], out_sem.at[j])
        )
        outs[-1].start()
    gg_ref[...] = jnp.broadcast_to(gate_sum, (rows, 128)).T[0:1]

    for copy in nos:
        copy.wait_recv()
    for copy in outs:
        copy.wait()
    for copy in drains:
        copy.wait_send()


def publish_kernel(*refs):
    count = 3
    sources, targets, held = refs[:count], refs[count:2 * count], refs[2 * count:3 * count]
    into, out = refs[3 * count:]
    ins = [pltpu.make_async_copy(sources[i], held[i], into.at[i]) for i in range(count)]
    outs = [pltpu.make_async_copy(held[i], targets[i], out.at[i]) for i in range(count)]
    for copy in ins:
        copy.start()
    for i in (0, 2, 1):
        ins[i].wait()
        outs[i].start()
    for copy in outs:
        copy.wait()


def publish(*arrays):
    hbm = pl.BlockSpec(memory_space=pl.ANY)
    return pl.pallas_call(
        publish_kernel,
        out_shape=tuple(jax.ShapeDtypeStruct(a.shape, a.dtype) for a in arrays),
        in_specs=[hbm] * len(arrays),
        out_specs=(hbm,) * len(arrays),
        scratch_shapes=[pltpu.VMEM(a.shape, a.dtype) for a in arrays]
        + [pltpu.SemaphoreType.DMA((len(arrays),))] * 2,
    )(*arrays)


def dense_body(
    hidden_fwd, down_weight, residual, route_fwd, gate_fwd, hidden_bwd, route_bwd, gate_bwd, upstream
):
    n = lax.axis_size("expert")
    sections = lax.axis_size("section")
    _, rows, ff = hidden_fwd.shape
    d = down_weight.shape[2]
    tokens, top = route_fwd.shape[1:]
    chips = n // 2
    nch, nag, nbw = 4, 2, 3
    half = chips * tokens
    dma = pltpu.SemaphoreType.DMA
    hbm = pl.BlockSpec(memory_space=pl.ANY)
    results = pl.pallas_call(
        functools.partial(kernel, n, sections, nch, nag, nbw),
        out_shape=(
            jax.ShapeDtypeStruct((1, tokens, d), BF16),
            jax.ShapeDtypeStruct((1, rows, ff), BF16),
            jax.ShapeDtypeStruct((1, rows), F32),
        ),
        in_specs=[hbm] * 9,
        out_specs=(hbm, hbm, pl.BlockSpec(memory_space=pltpu.VMEM)),
        scratch_shapes=[
            pltpu.VMEM((rows, ff), BF16),
            pltpu.VMEM((ff, d), BF16),
            pltpu.VMEM((tokens, d), BF16),
            pltpu.VMEM((rows, ff), BF16),
            pltpu.VMEM((2, top, tokens), jnp.int32),
            pltpu.VMEM((2, top, tokens), F32),
            pltpu.VMEM((top, 4 * tokens), F32),
            pltpu.VMEM((n, top, 4 * tokens), F32),
            pltpu.VMEM((2, chips, tokens, d), BF16),
            pltpu.VMEM((rows, d), BF16),
            pltpu.VMEM((half, d), F32),
            pltpu.VMEM((half, d), BF16),
            pltpu.VMEM((half, d), BF16),
            pltpu.VMEM((half, d), BF16),
            pltpu.VMEM((tokens, d), BF16),
            pltpu.VMEM((tokens, d), BF16),
            pltpu.VMEM((tokens, d), BF16),
            pltpu.VMEM((tokens, d), BF16),
            pltpu.VMEM((tokens, d), BF16),
            pltpu.VMEM((rows, ff), BF16),
            dma((nch + 3,)),
            dma((4,)),
            dma((n - 1,)),
            dma((n - 1,)),
            dma((nag,)),
            dma((nag,)),
            dma((3, nag)),
            dma((3, nag)),
            dma((4, nag)),
            dma((4, nag)),
            dma((nch,)),
            dma((nch,)),
            dma((3, nch)),
            dma((3, nch)),
            dma((nch,)),
            dma((nch,)),
            dma((nbw,)),
        ],
        compiler_params=pltpu.CompilerParams(
            collective_id=0, has_side_effects=True, vmem_limit_bytes=60 << 20
        ),
    )(
        hidden_fwd, down_weight, residual, route_fwd[0].T, gate_fwd[0].T, hidden_bwd,
        route_bwd[0].T, gate_bwd[0].T, upstream,
    )
    return publish(*results)


def body(*args):
    n = lax.axis_size("expert")
    dense = args[3].shape[2] == n and n // 2 == 4 and lax.axis_size("section") > 2
    return (dense_body if dense else sparse_body)(*args)


def solution(mesh):
    wide = P("section", "expert", None)
    return jax.shard_map(
        body,
        mesh=mesh,
        in_specs=(wide, P("expert", None, None), wide, wide, wide, wide, wide, wide, wide),
        out_specs=(wide, wide, P("section", "expert")),
        check_vma=False,
    )
```

```python
import functools

import jax
import jax.numpy as jnp
from jax import lax
from jax.experimental import pallas as pl
from jax.experimental.pallas import tpu as pltpu
from jax.sharding import PartitionSpec as P

F32 = jnp.float32
BF16 = jnp.bfloat16


def from_behind(block, axis, distance):
    devices = range(lax.axis_size(axis))
    route = [((i - distance) % len(devices), i) for i in devices]
    return lax.ppermute(block, axis, route)


def forward_local(hidden_fwd, down_weight):
    return jnp.dot(hidden_fwd[0], down_weight[0], preferred_element_type=F32).astype(BF16)


def combine_rows(returned, route_fwd, gate_fwd, residual):
    picked_rows = returned[route_fwd[0]]
    combined = residual[0].astype(F32) + jnp.sum(gate_fwd[0][:, :, None] * picked_rows, axis=1)
    return combined.astype(BF16)


def dispatch_rows(grad_in, route_bwd, gate_bwd):
    top = route_bwd.shape[-1]
    flat_slots = route_bwd[0].reshape(-1)
    route_count = flat_slots.shape[0]
    anchor = (
        jnp.zeros((route_count,), jnp.int32)
        .at[flat_slots]
        .set(jnp.arange(route_count, dtype=jnp.int32))
    )
    outgoing = grad_in[0][anchor // top]
    weight_rows = gate_bwd[0].reshape(-1)[anchor].astype(BF16)
    return (outgoing, weight_rows)


def backward_local(received, weights_in, hidden_bwd, down_weight):
    grad_hidden = lax.dot_general(
        received, down_weight[0], (((1,), (1,)), ((), ())), preferred_element_type=F32
    )
    gate_grad = jnp.sum(hidden_bwd[0] * grad_hidden, axis=1)
    hidden_grad = (weights_in.astype(F32)[:, None] * grad_hidden).astype(BF16)
    return (hidden_grad[None], gate_grad[None])


def sparse_body(
    hidden_fwd, down_weight, residual, route_fwd, gate_fwd, hidden_bwd, route_bwd, gate_bwd, upstream
):
    grad_in = from_behind(upstream, "section", -1)
    outgoing, weight_rows = dispatch_rows(grad_in, route_bwd, gate_bwd)
    projected = forward_local(hidden_fwd, down_weight)
    returned = lax.all_to_all(projected, "expert", split_axis=0, concat_axis=0, tiled=True)
    received, weights_in = (
        lax.all_to_all(outgoing, "expert", split_axis=0, concat_axis=0, tiled=True),
        lax.all_to_all(weight_rows, "expert", split_axis=0, concat_axis=0, tiled=True),
    )
    layer_out = combine_rows(returned, route_fwd, gate_fwd, residual)
    next_input = from_behind(layer_out[None], "section", 1)
    hidden_grad, gate_grad = backward_local(received, weights_in, hidden_bwd, down_weight)
    return (next_input, hidden_grad, gate_grad)


def kernel(
    n, sections, nch, nag, nbw,
    hf_ref, w_ref, res_ref, rf_ref, gf_ref, hb_ref, rb_ref, gb_ref, up_ref,
    next_ref, hg_ref, gg_ref,
    up, hf, w, res, hb, ti, tf, pack, tab, gbuf, gp, cown, csend, crecv, ssend, smid, r1a, r1b, r2,
    nout, hgs,
    ld, sm_loc, sm_send, sm_recv, z_send, z_recv, ag_send, ag_recv, fw_send, fw_recv,
    xc_send, xc_recv, rs_send, rs_recv, no_send, no_recv, out_sem,
):
    e = lax.axis_index("expert")
    s = lax.axis_index("section")
    chips = n // 2
    p = lax.div(e, 2)
    c = lax.rem(e, 2)
    mine = c * chips + p
    partner = e + 1 - 2 * c
    above = lax.rem(s + 1, sections)
    below = lax.rem(s + sections - 1, sections)
    beside_x = p + 1 - 2 * lax.rem(p, 2)
    beside_y = lax.rem(p + 2, chips)
    across = chips - 1 - p
    rows, ff = hf.shape
    d = w.shape[1]
    tokens = res.shape[0]
    cap = rows // n
    half = chips * tokens
    dc = d // nch
    ta = tokens // nag
    fb = ff // nbw

    def cols(i):
        return slice(i * dc, (i + 1) * dc)

    def part(i):
        return slice(i * ta, (i + 1) * ta)

    def of_chip(q):
        return pl.ds(pl.multiple_of(q * tokens, tokens), tokens)

    def remote(src, dst, ss, rs, section=None, expert=None):
        return pltpu.make_async_remote_copy(
            src_ref=src, dst_ref=dst, send_sem=ss, recv_sem=rs,
            device_id={
                "section": s if section is None else section,
                "expert": e if expert is None else expert,
            },
            device_id_type=pl.DeviceIdType.MESH,
        )

    barrier = pltpu.get_barrier_semaphore()
    for k in range(1, n):
        pl.semaphore_signal(
            barrier, inc=1, device_id={"section": s, "expert": lax.rem(e + k, n)},
            device_id_type=pl.DeviceIdType.MESH,
        )
    for other in (above, below):
        pl.semaphore_signal(
            barrier, inc=1, device_id={"section": other, "expert": e},
            device_id_type=pl.DeviceIdType.MESH,
        )
    local = [pltpu.make_async_copy(up_ref.at[0], up, sm_loc.at[4])]
    local[0].start()
    for i, (src, dst) in enumerate(
        [(rf_ref, ti.at[0]), (gf_ref, tf.at[0]), (rb_ref, ti.at[1]), (gb_ref, tf.at[1])]
    ):
        local.append(pltpu.make_async_copy(src, dst, sm_loc.at[i]))
        local[-1].start()
    loads = [pltpu.make_async_copy(hf_ref.at[0], hf, ld.at[nch])]
    for i in range(nch):
        loads.append(
            pltpu.make_async_copy(w_ref.at[0, :, cols(i)], w.at[:, cols(i)], ld.at[i])
        )
    loads.append(pltpu.make_async_copy(res_ref.at[0], res, ld.at[nch + 1]))
    loads.append(pltpu.make_async_copy(hb_ref.at[0], hb, ld.at[nch + 2]))
    for copy in local:
        copy.wait()
    packed = jnp.concatenate([ti[0].astype(F32), tf[0], ti[1].astype(F32), tf[1]], axis=1)
    pack[...] = packed
    tab[mine] = packed
    pl.semaphore_wait(barrier, n + 1)

    drains = []

    def send(copy):
        copy.start()
        drains.append(copy)
        return copy

    zs = []
    for i in range(nag):
        zs.append(
            send(remote(up.at[part(i)], gbuf.at[c, p, part(i)],
                        z_send.at[i], z_recv.at[i], section=below))
        )
    small = []
    for k in range(1, n):
        small.append(
            send(remote(pack, tab.at[mine], sm_send.at[k - 1], sm_recv.at[k - 1],
                        expert=lax.rem(e + k, n)))
        )

    for load in loads:
        load.start()

    def expert_at(q):
        return 2 * q + c

    def block(q, i, core=None):
        return gbuf.at[c if core is None else core, q, part(i)]

    def gather(q, j, i, to):
        ref = block(q, i)
        return remote(ref, ref, ag_send.at[j, i], ag_recv.at[j, i], expert=expert_at(to))

    def hand_over(q, j, i, core=None):
        ref = block(q, i, core)
        return remote(ref, ref, fw_send.at[j, i], fw_recv.at[j, i], expert=partner)

    def gather_out(i):
        zs[i].wait_recv()
        send(gather(p, 0, i, beside_x))
        send(gather(p, 1, i, beside_y))
        send(hand_over(p, 0, i))

    def gather_near(i):
        gather(beside_x, 0, i, beside_x).wait_recv()
        if i % 2 == 0:
            send(gather(beside_x, 2, i, beside_y))
        send(hand_over(beside_x, 1, i))
        gather(beside_y, 1, i, beside_y).wait_recv()
        if i % 2 == 1:
            send(gather(beside_y, 2, i, beside_x))
        send(hand_over(beside_y, 2, i))

    def gather_far(i):
        gather(across, 2, i, beside_x).wait_recv()
        send(hand_over(across, 3, i))

    def gather_done(i):
        for j, q in enumerate((p, beside_x, beside_y, across)):
            hand_over(q, j, i, 1 - c).wait_recv()

    def project(i):
        loads[1 + i].wait()
        return jnp.dot(hf[...], w[:, cols(i)], preferred_element_type=F32).astype(BF16)

    loads[0].wait()
    out = project(0)
    for copy in small:
        copy.wait_recv()

    def table(kind):
        span = slice(kind * tokens, (kind + 1) * tokens)
        return jnp.concatenate([tab[q, :, span] for q in range(n)], axis=1)

    lo = e * cap
    lane = lax.broadcasted_iota(jnp.int32, (1, n * tokens), 1)
    lane_q = lane // tokens
    lane_base = (2 * (lane_q % chips) + lane_q // chips) * cap

    route = table(0).astype(jnp.int32)
    hit = (route >= lo) & (route < lo + cap)
    pos = jnp.where(hit, route - lo, 0).astype(F32).T
    gate_col = jnp.sum(jnp.where(hit, table(1), 0.0).T, axis=1, keepdims=True)
    row = lax.broadcasted_iota(jnp.int32, (n * tokens, 1), 0)
    row_q = row // tokens
    want = (2 * (row_q % chips) + row_q // chips) * cap + jnp.sum(
        pos, axis=1, keepdims=True
    ).astype(jnp.int32)
    pick = jnp.where(
        lax.broadcasted_iota(jnp.int32, (n * tokens, rows), 1) == want, 1.0, 0.0
    ).astype(BF16)

    def weigh(i, out):
        got = gate_col * jnp.dot(pick, out, preferred_element_type=F32)
        low, high = got[:half], got[half:]
        cown[:, cols(i)] = jnp.where(c == 0, low, high)
        csend[:, cols(i)] = jnp.where(c == 0, high, low).astype(BF16)
        return send(
            remote(csend.at[:, cols(i)], crecv.at[:, cols(i)], xc_send.at[i], xc_recv.at[i],
                   expert=partner)
        )

    def first_second(i):
        return (beside_x, beside_y) if i % 2 == 0 else (beside_y, beside_x)

    far, near, last, nos = {}, {}, {}, []

    def scatter_out(i):
        first, _ = first_second(i)
        pairs[i].wait_recv()
        total = cown[:, cols(i)] + crecv[:, cols(i)].astype(F32)
        cown[:, cols(i)] = total
        ssend[:, cols(i)] = total.astype(BF16)
        far[i] = send(remote(ssend.at[of_chip(across), cols(i)], r1a.at[:, cols(i)],
                             rs_send.at[0, i], rs_recv.at[0, i], expert=expert_at(first)))
        near[i] = send(remote(ssend.at[of_chip(first), cols(i)], r1b.at[:, cols(i)],
                              rs_send.at[1, i], rs_recv.at[1, i], expert=expert_at(first)))

    def scatter_mid(i):
        _, second = first_second(i)
        far[i].wait_recv()
        both = cown[of_chip(second), cols(i)] + r1a[:, cols(i)].astype(F32)
        smid[:, cols(i)] = both.astype(BF16)
        last[i] = send(remote(smid.at[:, cols(i)], r2.at[:, cols(i)],
                              rs_send.at[2, i], rs_recv.at[2, i], expert=expert_at(second)))

    def finish(i):
        near[i].wait_recv()
        total = res[:, cols(i)].astype(F32) + cown[of_chip(p), cols(i)]
        total = total + r1b[:, cols(i)].astype(F32)
        last[i].wait_recv()
        total = total + r2[:, cols(i)].astype(F32)
        nout[:, cols(i)] = total.astype(BF16)
        nos.append(
            send(remote(nout.at[:, cols(i)], next_ref.at[0, :, cols(i)],
                        no_send.at[i], no_recv.at[i], section=above))
        )

    pairs = []
    for i in range(nch):
        if i:
            out = project(i)
        pairs.append(weigh(i, out))
        if i >= 1:
            scatter_out(i - 1)
        if i < nag:
            gather_out(i)
    scatter_out(nch - 1)
    for i in range(nag):
        gather_near(i)
    for i in range(nch):
        scatter_mid(i)
    for i in range(nag):
        gather_far(i)

    route = table(2).astype(jnp.int32)
    hit = (route >= lo) & (route < lo + cap)
    slot = jnp.sum(jnp.where(hit, route - lo, 0), axis=0, keepdims=True)
    gate_row = jnp.sum(jnp.where(hit, table(3), 0.0), axis=0, keepdims=True)
    match = lax.broadcasted_iota(jnp.int32, (rows, n * tokens), 0) == lane_base + slot
    weight_col = jnp.sum(jnp.where(match, gate_row, 0.0), axis=1, keepdims=True)
    weight_col = weight_col.astype(BF16).astype(F32)
    place = jnp.where(match, 1.0, 0.0).astype(BF16)

    loads[nch + 1].wait()
    loads[nch + 2].wait()
    for i in range(nch):
        finish(i)
    for i in range(nag):
        gather_done(i)
    for i in range(nch):
        tok = gbuf[:, :, :, cols(i)].reshape(n * tokens, dc)
        gp[:, cols(i)] = jnp.dot(place, tok, preferred_element_type=F32).astype(BF16)

    outs = []
    gate_sum = jnp.zeros((rows, 1), F32)
    for j in range(nbw):
        span = slice(j * fb, (j + 1) * fb)
        grad = lax.dot_general(
            gp[...], w[span, :], (((1,), (1,)), ((), ())), preferred_element_type=F32
        )
        gate_sum = gate_sum + jnp.sum(hb[:, span].astype(F32) * grad, axis=1, keepdims=True)
        hgs[:, span] = (weight_col * grad).astype(BF16)
        outs.append(
            pltpu.make_async_copy(hgs.at[:, span], hg_ref.at[0, :, span], out_sem.at[j])
        )
        outs[-1].start()
    gg_ref[...] = jnp.broadcast_to(gate_sum, (rows, 128)).T[0:1]

    for copy in nos:
        copy.wait_recv()
    for copy in outs:
        copy.wait()
    for copy in drains:
        copy.wait_send()


def publish_kernel(*refs):
    count = 3
    sources, targets, held = refs[:count], refs[count:2 * count], refs[2 * count:3 * count]
    into, out = refs[3 * count:]
    ins = [pltpu.make_async_copy(sources[i], held[i], into.at[i]) for i in range(count)]
    outs = [pltpu.make_async_copy(held[i], targets[i], out.at[i]) for i in range(count)]
    for copy in ins:
        copy.start()
    for i in (0, 2, 1):
        ins[i].wait()
        outs[i].start()
    for copy in outs:
        copy.wait()


def publish(*arrays):
    hbm = pl.BlockSpec(memory_space=pl.ANY)
    return pl.pallas_call(
        publish_kernel,
        out_shape=tuple(jax.ShapeDtypeStruct(a.shape, a.dtype) for a in arrays),
        in_specs=[hbm] * len(arrays),
        out_specs=(hbm,) * len(arrays),
        scratch_shapes=[pltpu.VMEM(a.shape, a.dtype) for a in arrays]
        + [pltpu.SemaphoreType.DMA((len(arrays),))] * 2,
    )(*arrays)


def dense_body(
    hidden_fwd, down_weight, residual, route_fwd, gate_fwd, hidden_bwd, route_bwd, gate_bwd, upstream
):
    n = lax.axis_size("expert")
    sections = lax.axis_size("section")
    _, rows, ff = hidden_fwd.shape
    d = down_weight.shape[2]
    tokens, top = route_fwd.shape[1:]
    chips = n // 2
    nch, nag, nbw = 4, 2, 3
    half = chips * tokens
    dma = pltpu.SemaphoreType.DMA
    hbm = pl.BlockSpec(memory_space=pl.ANY)
    results = pl.pallas_call(
        functools.partial(kernel, n, sections, nch, nag, nbw),
        out_shape=(
            jax.ShapeDtypeStruct((1, tokens, d), BF16),
            jax.ShapeDtypeStruct((1, rows, ff), BF16),
            jax.ShapeDtypeStruct((1, rows), F32),
        ),
        in_specs=[hbm] * 9,
        out_specs=(hbm, hbm, pl.BlockSpec(memory_space=pltpu.VMEM)),
        scratch_shapes=[
            pltpu.VMEM((tokens, d), BF16),
            pltpu.VMEM((rows, ff), BF16),
            pltpu.VMEM((ff, d), BF16),
            pltpu.VMEM((tokens, d), BF16),
            pltpu.VMEM((rows, ff), BF16),
            pltpu.VMEM((2, top, tokens), jnp.int32),
            pltpu.VMEM((2, top, tokens), F32),
            pltpu.VMEM((top, 4 * tokens), F32),
            pltpu.VMEM((n, top, 4 * tokens), F32),
            pltpu.VMEM((2, chips, tokens, d), BF16),
            pltpu.VMEM((rows, d), BF16),
            pltpu.VMEM((half, d), F32),
            pltpu.VMEM((half, d), BF16),
            pltpu.VMEM((half, d), BF16),
            pltpu.VMEM((half, d), BF16),
            pltpu.VMEM((tokens, d), BF16),
            pltpu.VMEM((tokens, d), BF16),
            pltpu.VMEM((tokens, d), BF16),
            pltpu.VMEM((tokens, d), BF16),
            pltpu.VMEM((tokens, d), BF16),
            pltpu.VMEM((rows, ff), BF16),
            dma((nch + 3,)),
            dma((5,)),
            dma((n - 1,)),
            dma((n - 1,)),
            dma((nag,)),
            dma((nag,)),
            dma((3, nag)),
            dma((3, nag)),
            dma((4, nag)),
            dma((4, nag)),
            dma((nch,)),
            dma((nch,)),
            dma((3, nch)),
            dma((3, nch)),
            dma((nch,)),
            dma((nch,)),
            dma((nbw,)),
        ],
        compiler_params=pltpu.CompilerParams(
            collective_id=0, has_side_effects=True, vmem_limit_bytes=60 << 20
        ),
    )(
        hidden_fwd, down_weight, residual, route_fwd[0].T, gate_fwd[0].T, hidden_bwd,
        route_bwd[0].T, gate_bwd[0].T, upstream,
    )
    return publish(*results)


def body(*args):
    n = lax.axis_size("expert")
    dense = args[3].shape[2] == n and n // 2 == 4 and lax.axis_size("section") > 2
    return (dense_body if dense else sparse_body)(*args)


def solution(mesh):
    wide = P("section", "expert", None)
    return jax.shard_map(
        body,
        mesh=mesh,
        in_specs=(wide, P("expert", None, None), wide, wide, wide, wide, wide, wide, wide),
        out_specs=(wide, wide, P("section", "expert")),
        check_vma=False,
    )
```
